256 devices in a mesh: dp: 16 (over x, y_hi, core), ctx: 16 (over z, y_lo).
Axes of the slice: x: 4, y: 4 (y_hi: 2, y_lo: 2; y = y_hi * 2 + y_lo), z: 8, core: 2. Of those that a mesh axis runs over, the one named last changes fastest.
Arguments:
- query_frames: bfloat16 [65536, 2560], P(('dp', 'ctx')), parts along dimension 0, may hold values from -8 to 8
- key_frames: bfloat16 [65536, 2560], P(('dp', 'ctx')), parts along dimension 0, may hold values from -8 to 8
- value_frames: bfloat16 [65536, 2560], P(('dp', 'ctx')), parts along dimension 0, may hold values from -6 to 6
- stream: bfloat16 [65536, 5120], P(('dp', 'ctx')), parts along dimension 0, may hold values from -1.25 to 1.25
- out_weight: bfloat16 [2560, 5120], P('ctx'), may hold values from -0.125 to 0.125
Outputs:
- layer_out: bfloat16 [65536, 5120], P(('dp', 'ctx')), parts along dimension 0
The draws below stay inside these ranges and needn't reach their ends.
There are 16 independent parts, one for each index of `dp`. The reference program is written for one: setup_inputs(seed, part) draws one part's arguments, and reference() takes and returns one part's arrays. A program takes and returns all parts, laid end to end along the dimension named above; an argument that names none is the same for every part. Nothing has to cross between parts.
All inputs are finite; a program needn't handle non-finite values.
Results may differ from the reference program's by a relative error of at most 0.01.
Values may be sent and summed in bfloat16 or wider, within the bound.
A program may use at most 128 MiB of HBM per device.

```python
import jax
import jax.numpy as jnp
from jax import lax

D = 5120
HEADS = 20
HEAD_SIZE = 128
TOK_DEV = 256
TOKENS = 4096


def draw_query_frames(key, part):
    result = jnp.clip(jax.random.normal(jax.random.fold_in(key, 1), (TOKENS, HEADS * HEAD_SIZE), jnp.float32), -6.0, 6.0)
    return result.astype(jnp.bfloat16)


def draw_key_frames(key, part):
    result = jnp.clip(jax.random.normal(jax.random.fold_in(key, 2), (TOKENS, HEADS * HEAD_SIZE), jnp.float32), -6.0, 6.0)
    return result.astype(jnp.bfloat16)


def shard_levels(rng, dims, shards, low, high):
    def one(axis_at, parts):
        draws = jax.random.uniform(jax.random.fold_in(jax.random.fold_in(rng, 6), axis_at), (parts,), jnp.float32, low / len(shards), high / len(shards))
        return jnp.repeat(jnp.exp(draws), dims[axis_at] // parts).reshape((-1,) + (1,) * (len(dims) - axis_at - 1))

    factor_of = one(*shards[0])
    for cut in shards[1:]:
        factor_of = factor_of * one(*cut)
    return factor_of


def centred(stream_key, shape, width, most, pieces=(), kind=jnp.bfloat16):
    gain = shard_levels(stream_key, shape, pieces, -0.22, 0.18) if pieces else 1.0
    drawn = jax.random.normal(stream_key, shape, jnp.float32) * width * gain
    return jnp.minimum(jnp.maximum(drawn, -most), most).astype(kind)


def setup_inputs(seed: int = 0, part: int = 0) -> dict:
    seeds = jax.random.split(jax.random.key(seed), 6)
    part_splits = jax.random.split(jax.random.fold_in(seeds[5], part), 6)
    query_frames = draw_query_frames(jax.random.fold_in(jax.random.fold_in(seeds[5], part), 71), part)
    key_frames = draw_key_frames(jax.random.fold_in(jax.random.fold_in(seeds[5], part), 71), part)
    value_frames = centred(part_splits[2], (TOKENS, HEADS * HEAD_SIZE), 1.0, 6.0, ((0, 16),))
    stream = centred(part_splits[3], (TOKENS, D), 0.08, 1.25, ((0, 16),))
    out_weight = centred(seeds[4], (HEADS * HEAD_SIZE, D), (HEADS * HEAD_SIZE) ** -0.5, 0.125, ((0, 16),))
    return dict(query_frames=query_frames, key_frames=key_frames, value_frames=value_frames, stream=stream, out_weight=out_weight)


def attend_block(blocks):
    query_block, key_window, value_window, block_index = blocks
    count = TOKENS // TOK_DEV
    earlier_ok = jnp.broadcast_to(block_index > 0, (TOK_DEV,))
    middle_ok = jnp.ones((TOK_DEV,), dtype=bool)
    later_ok = jnp.broadcast_to(block_index < count - 1, (TOK_DEV,))
    valid = jnp.concatenate([earlier_ok, middle_ok, later_ok])
    scores = jnp.einsum("qhd,khd->hqk", query_block.astype(jnp.float32), key_window.astype(jnp.float32)) * (HEAD_SIZE ** -0.5)
    scores = jnp.where(valid[None, None, :], scores, -1e30)
    largest = jnp.max(scores, axis=2, keepdims=True)
    expon = jnp.exp(scores - largest)
    probs = (expon / jnp.sum(expon, axis=2, keepdims=True)).astype(jnp.bfloat16)
    context = jnp.einsum("hqk,khd->qhd", probs.astype(jnp.float32), value_window.astype(jnp.float32))
    return context.astype(jnp.bfloat16).reshape(TOK_DEV, HEADS * HEAD_SIZE)


def reference(query_frames, key_frames, value_frames, stream, out_weight):
    blocks = TOKENS // TOK_DEV
    query_blocks = query_frames.reshape(blocks, TOK_DEV, HEADS, HEAD_SIZE)
    key_blocks = key_frames.reshape(blocks, TOK_DEV, HEADS, HEAD_SIZE)
    value_blocks = value_frames.reshape(blocks, TOK_DEV, HEADS, HEAD_SIZE)
    key_window = jnp.concatenate([jnp.roll(key_blocks, 1, axis=0), key_blocks, jnp.roll(key_blocks, -1, axis=0)], axis=1)
    value_window = jnp.concatenate([jnp.roll(value_blocks, 1, axis=0), value_blocks, jnp.roll(value_blocks, -1, axis=0)], axis=1)
    block_ids = jnp.arange(blocks, dtype=jnp.int32)
    context = lax.map(attend_block, (query_blocks, key_window, value_window, block_ids)).reshape(TOKENS, HEADS * HEAD_SIZE)
    product = jnp.dot(context, out_weight, preferred_element_type=jnp.float32)
    return (stream.astype(jnp.float32) + product).astype(jnp.bfloat16)
```

```python
import jax
import jax.numpy as jnp
from jax import lax
from jax.experimental import pallas as pl
from jax.experimental.pallas import tpu as pltpu
from jax.sharding import PartitionSpec as P

HEADS = 20
HEAD_SIZE = 128
BLOCK = 256
WIDTH = 2560
D = 5120
SHARD = 160
ROWS = 80
COLS = 1280
GROUPS = 10
TICKS = 14
SCALE = HEAD_SIZE ** (-0.5) * 1.4426950408889634
MESH = pl.DeviceIdType.MESH


def kernel(
    q_hbm, k_hbm, v_hbm, stream_hbm, w_hbm, out_hbm,
    q, own, near, far, ctx, stream, weight, out,
    in_sem, z_send, z_recv, h_send, h_recv, y_send, y_recv, x_send, x_recv,
    d_send, d_recv, c_send, c_recv, near_send, near_recv, far_send, far_recv, out_sem,
):
    dp = lax.axis_index("dp")
    at = lax.axis_index("ctx")
    core = lax.rem(dp, 2)
    x = lax.div(dp, 4)
    y_hi = lax.rem(lax.div(dp, 2), 2)
    z = lax.div(at, 2)
    par = lax.rem(at, 2)
    sig = 1 - 2 * par
    mine = lax.rem(x, 2)

    def plane(step):
        return lax.rem(z + step + 16, 8)

    z_out = (dp, plane(-sig) * 2 + par)
    h_out = (dp, plane(sig) * 2 + par)
    y_far = (dp + 2 - 4 * y_hi, at + 1 - 2 * par)
    y_near = (dp, at + 1 - 2 * par)
    other = (dp + 1 - 2 * core, at)

    def x_dev(r):
        return (lax.rem(dp + 4 + 8 * r, 16), at)

    barrier = pltpu.get_barrier_semaphore()
    for dev in (z_out, h_out, y_far, y_near, other, x_dev(0), x_dev(1)):
        pl.semaphore_signal(barrier, inc=1, device_id=dev, device_id_type=MESH)
    pl.semaphore_wait(barrier, 7)

    def piece(parity, zz, half, r):
        row = pl.multiple_of(SHARD * (2 * zz + parity) + ROWS * r, 16)
        col = pl.multiple_of(core * WIDTH + half * COLS, COLS)
        return weight.at[pl.ds(row, ROWS), pl.ds(col, COLS)]

    def source(half, r):
        row = pl.multiple_of(ROWS * r, 16)
        col = pl.multiple_of(core * WIDTH + half * COLS, COLS)
        return w_hbm.at[pl.ds(row, ROWS), pl.ds(col, COLS)]

    def remote(src, dst, send, recv, dev):
        return pltpu.make_async_remote_copy(
            src_ref=src, dst_ref=dst, send_sem=send, recv_sem=recv, device_id=dev, device_id_type=MESH
        )

    def spot(parity, zz, r):
        return piece(parity, zz, mine, r)

    def z_spot(t, half):
        early = t < 12
        step = jnp.where(early, sig * (1 + lax.div(t, 2)), -6 * sig)
        return piece(jnp.where(early, par, 1 - par), plane(step), half, lax.rem(t, 2))

    def h_spot(t, half):
        return piece(par, plane(-sig), half, 1 - t)

    def y_spot(t, half):
        n = lax.div(t, 2)
        k = jnp.where(n == 0, 0, jnp.where(n == 1, 7, n - 1))
        return piece(1 - par, plane(-sig * k), half, 1 - lax.rem(t, 2))

    def x_spot(r, t, half):
        by_z = lax.rem(t, 2) == r
        n = lax.div(t, 2)
        z_step = jnp.where(t < 12, sig * (1 + n), -6 * sig)
        y_step = jnp.where(t < 2, -sig, -sig * jnp.where(n == 1, 7, n - 1))
        z_par = jnp.where(t < 12, par, 1 - par)
        y_par = jnp.where(t < 2, par, 1 - par)
        return piece(jnp.where(by_z, z_par, y_par), plane(jnp.where(by_z, z_step, y_step)), half, r)

    def pass_over(ref, i):
        remote(ref, ref, c_send.at[i], c_recv.at[i], other).start()

    def arrived(ref, send, recv):
        remote(ref, ref, send, recv, other).wait_recv()

    def kv(ref_k, ref_v, which, g):
        cols = pl.ds(pl.multiple_of(g * 256, 256), 256)
        return (ref_k if which == 0 else ref_v).at[:, cols]

    def slot(buf, which, g):
        return buf.at[which, :, pl.ds(pl.multiple_of(g * 256, 256), 256)]

    def start_near(g):
        for which in range(2):
            remote(
                kv(k_hbm, v_hbm, which, g), slot(near, which, g),
                near_send.at[which, g], near_recv.at[which, g], y_near,
            ).start()

    start_near(0)
    for i in range(2):
        home = piece(par, z, mine, i)
        remote(source(mine, i), home, z_send.at[i], z_recv.at[i], z_out).start()
        home = piece(par, z, mine, 1 - i)
        remote(source(mine, 1 - i), home, h_send.at[i], h_recv.at[i], h_out).start()
        remote(source(mine, 1 - i), home, y_send.at[i], y_recv.at[i], y_far).start()

    @pl.loop(1, GROUPS)
    def _(g):
        start_near(g)

    for i in range(2):
        home = piece(par, z, 1 - mine, i)
        remote(source(1 - mine, i), home, d_send.at[i], d_recv.at[i], y_near).start()

    loads = [
        pltpu.make_async_copy(q_hbm, q, in_sem.at[0]),
        pltpu.make_async_copy(k_hbm, own.at[0], in_sem.at[1]),
        pltpu.make_async_copy(v_hbm, own.at[1], in_sem.at[2]),
        pltpu.make_async_copy(
            w_hbm, weight.at[pl.ds(pl.multiple_of(SHARD * at, 16), SHARD), :], in_sem.at[3]
        ),
        pltpu.make_async_copy(stream_hbm, stream, in_sem.at[4]),
    ]
    for load in loads:
        load.start()
    for load in loads:
        load.wait()

    bias = jnp.where((z + par > 0) & (z + par < 8), 0.0, -1e30).astype(jnp.float32)
    ones = jnp.ones((BLOCK, HEAD_SIZE), jnp.bfloat16)

    def attend(h):
        cols = pl.ds(pl.multiple_of(h * HEAD_SIZE, HEAD_SIZE), HEAD_SIZE)
        query = q[:, cols]

        def score(buf):
            return lax.dot_general(
                query, buf[0, :, cols], (((1,), (1,)), ((), ())), preferred_element_type=jnp.float32
            )

        scores = [score(own), score(near), score(far) + bias]
        largest = jnp.maximum(jnp.maximum(scores[0], scores[1]), scores[2]).max(axis=1, keepdims=True)
        total = None
        for buf, s in zip((own, near, far), scores):
            expon = jnp.exp2((s - largest) * SCALE).astype(jnp.bfloat16)
            values = jnp.concatenate([buf[1, :, cols], ones], axis=1)
            part = jnp.dot(expon, values, preferred_element_type=jnp.float32)
            total = part if total is None else total + part
        ctx[:, cols] = (total[:, :HEAD_SIZE] / total[:, HEAD_SIZE:]).astype(jnp.bfloat16)

    @pl.loop(0, TICKS + 1)
    def _(t):
        @pl.when(t < TICKS)
        def _():
            got = z_spot(t, mine)
            arrived(got, z_send.at[t], z_recv.at[t])

            @pl.when(t < 12)
            def _():
                k = jnp.where(t < 10, sig * (1 + lax.div(t, 2)), -7 * sig)
                ref = spot(jnp.where(t < 10, par, 1 - par), plane(k), lax.rem(t, 2))
                remote(ref, ref, z_send.at[t + 2], z_recv.at[t + 2], z_out).start()

            r = lax.rem(t, 2)
            remote(got, got, x_send.at[r, t], x_recv.at[r, t], x_dev(r)).start()
            pass_over(got, t)

            @pl.when(t < 2)
            def _():
                ref = h_spot(t, mine)
                arrived(ref, h_send.at[t], h_recv.at[t])
                remote(ref, ref, x_send.at[1 - r, t], x_recv.at[1 - r, t], x_dev(1 - r)).start()
                remote(ref, ref, y_send.at[t + 2], y_recv.at[t + 2], y_far).start()
                pass_over(ref, 14 + t)

            @pl.when((t > 0) & (t < 11))
            def _():
                ref = spot(par, plane(sig * (lax.div(t + 3, 2) - 1)), r)
                remote(ref, ref, y_send.at[t + 3], y_recv.at[t + 3], y_far).start()

            ref = y_spot(t, mine)
            arrived(ref, y_send.at[t], y_recv.at[t])

            @pl.when(t >= 2)
            def _():
                remote(ref, ref, x_send.at[1 - r, t], x_recv.at[1 - r, t], x_dev(1 - r)).start()

            pass_over(ref, 16 + t)

        @pl.loop(lax.div(t * 25, 32), jnp.minimum(lax.div((t + 1) * 25, 32), GROUPS))
        def _(g):
            for which in range(2):
                ref = slot(near, which, g)
                arrived(ref, near_send.at[which, g], near_recv.at[which, g])
                remote(ref, slot(far, which, g), far_send.at[which, g], far_recv.at[which, g], h_out).start()

        @pl.when(t >= 1)
        def _():
            for r in range(2):
                ref = x_spot(r, t - 1, 1 - mine)
                arrived(ref, x_send.at[r, t - 1], x_recv.at[r, t - 1])
                pass_over(ref, 30 + r * 14 + t - 1)

        def ready(s):
            return lax.div(jnp.maximum(s - 2, 0) * 25, 32)

        @pl.loop(ready(t), jnp.minimum(ready(t + 1), GROUPS))
        def _(g):
            for which in range(2):
                arrived(slot(far, which, g), far_send.at[which, g], far_recv.at[which, g])

            @pl.loop(0, 2)
            def _(i):
                attend(2 * g + i)

    for i in range(2):
        ref = piece(1 - par, z, 1 - mine, i)
        arrived(ref, d_send.at[i], d_recv.at[i])
        pass_over(ref, 58 + i)

    any_piece = weight.at[pl.ds(0, ROWS), pl.ds(0, COLS)]

    @pl.loop(0, 60)
    def _(i):
        arrived(any_piece, c_send.at[i], c_recv.at[i])

    def out_copy(n):
        cols = pl.ds(pl.multiple_of(n * 512, 512), 512)
        return pltpu.make_async_copy(out.at[:, cols], out_hbm.at[:, cols], out_sem.at[n])

    @pl.loop(0, 10)
    def _(n):
        cols = pl.ds(pl.multiple_of(n * 512, 512), 512)
        product = jnp.dot(ctx[...], weight[:, cols], preferred_element_type=jnp.float32)
        out[:, cols] = (stream[:, cols].astype(jnp.float32) + product).astype(jnp.bfloat16)
        out_copy(n).start()

    def sent(ref, send, recv):
        remote(ref, ref, send, recv, other).wait_send()

    @pl.loop(0, 14)
    def _(i):
        sent(any_piece, z_send.at[i], z_recv.at[i])
        sent(any_piece, y_send.at[i], y_recv.at[i])
        for r in range(2):
            sent(any_piece, x_send.at[r, i], x_recv.at[r, i])

    for i in range(2):
        sent(any_piece, h_send.at[i], h_recv.at[i])
        sent(any_piece, d_send.at[i], d_recv.at[i])

    @pl.loop(0, 60)
    def _(i):
        sent(any_piece, c_send.at[i], c_recv.at[i])

    @pl.loop(0, GROUPS)
    def _(g):
        for which in range(2):
            sent(slot(near, which, g), near_send.at[which, g], near_recv.at[which, g])
            sent(slot(far, which, g), far_send.at[which, g], far_recv.at[which, g])
        out_copy(g).wait()


def local(query_frames, key_frames, value_frames, stream, out_weight):
    dma = pltpu.SemaphoreType.DMA
    bf16 = jnp.bfloat16
    return pl.pallas_call(
        kernel,
        out_shape=jax.ShapeDtypeStruct((BLOCK, D), bf16),
        in_specs=[pl.BlockSpec(memory_space=pl.ANY)] * 5,
        out_specs=pl.BlockSpec(memory_space=pl.ANY),
        scratch_shapes=[
            pltpu.VMEM((BLOCK, WIDTH), bf16),
            pltpu.VMEM((2, BLOCK, WIDTH), bf16),
            pltpu.VMEM((2, BLOCK, WIDTH), bf16),
            pltpu.VMEM((2, BLOCK, WIDTH), bf16),
            pltpu.VMEM((BLOCK, WIDTH), bf16),
            pltpu.VMEM((BLOCK, D), bf16),
            pltpu.VMEM((WIDTH, D), bf16),
            pltpu.VMEM((BLOCK, D), bf16),
            dma((5,)),
            dma((14,)), dma((14,)),
            dma((2,)), dma((2,)),
            dma((14,)), dma((14,)),
            dma((2, 14)), dma((2, 14)),
            dma((2,)), dma((2,)),
            dma((60,)), dma((60,)),
            dma((2, GROUPS)), dma((2, GROUPS)),
            dma((2, GROUPS)), dma((2, GROUPS)),
            dma((10,)),
        ],
        compiler_params=pltpu.CompilerParams(
            collective_id=0, has_side_effects=True, vmem_limit_bytes=63 * 1024 * 1024
        ),
    )(query_frames, key_frames, value_frames, stream, out_weight)


def solution(mesh):
    in_specs = (
        P(("dp", "ctx"), None),
        P(("dp", "ctx"), None),
        P(("dp", "ctx"), None),
        P(("dp", "ctx"), None),
        P("ctx", None),
    )
    out_specs = P(("dp", "ctx"), None)
    return jax.shard_map(local, mesh=mesh, in_specs=in_specs, out_specs=out_specs, check_vma=False)
```

```python
import jax
import jax.numpy as jnp
from jax import lax
from jax.experimental import pallas as pl
from jax.experimental.pallas import tpu as pltpu
from jax.sharding import PartitionSpec as P

HEADS = 20
HEAD_SIZE = 128
BLOCK = 256
WIDTH = 2560
D = 5120
SHARD = 160
ROWS = 80
COLS = 1280
GROUPS = 10
TICKS = 14
LAST = 15
SCALE = HEAD_SIZE ** (-0.5) * 1.4426950408889634
MESH = pl.DeviceIdType.MESH


def kernel(
    q_hbm, k_hbm, v_hbm, stream_hbm, w_hbm, out,
    q, own, near, far, ctx, stream, weight, total,
    in_sem, z_send, z_recv, h_send, h_recv, y_send, y_recv, x_send, x_recv,
    d_send, d_recv, c_send, c_recv, near_send, near_recv, far_send, far_recv,
):
    dp = lax.axis_index("dp")
    at = lax.axis_index("ctx")
    core = lax.rem(dp, 2)
    x = lax.div(dp, 4)
    y_hi = lax.rem(lax.div(dp, 2), 2)
    z = lax.div(at, 2)
    par = lax.rem(at, 2)
    sig = 1 - 2 * par
    mine = lax.rem(x, 2)

    def plane(step):
        return lax.rem(z + step + 16, 8)

    z_out = (dp, plane(-sig) * 2 + par)
    h_out = (dp, plane(sig) * 2 + par)
    y_far = (dp + 2 - 4 * y_hi, at + 1 - 2 * par)
    y_near = (dp, at + 1 - 2 * par)
    other = (dp + 1 - 2 * core, at)

    def x_dev(r):
        return (lax.rem(dp + 4 + 8 * r, 16), at)

    barrier = pltpu.get_barrier_semaphore()
    for dev in (z_out, h_out, y_far, y_near, other, x_dev(0), x_dev(1)):
        pl.semaphore_signal(barrier, inc=1, device_id=dev, device_id_type=MESH)
    pl.semaphore_wait(barrier, 7)

    def piece(parity, zz, half, r):
        row = pl.multiple_of(SHARD * (2 * zz + parity) + ROWS * r, 16)
        col = pl.multiple_of(core * WIDTH + half * COLS, COLS)
        return weight.at[pl.ds(row, ROWS), pl.ds(col, COLS)]

    def source(half, r):
        row = pl.multiple_of(ROWS * r, 16)
        col = pl.multiple_of(core * WIDTH + half * COLS, COLS)
        return w_hbm.at[pl.ds(row, ROWS), pl.ds(col, COLS)]

    def remote(src, dst, send, recv, dev):
        return pltpu.make_async_remote_copy(
            src_ref=src, dst_ref=dst, send_sem=send, recv_sem=recv, device_id=dev, device_id_type=MESH
        )

    def spot(parity, zz, r):
        return piece(parity, zz, mine, r)

    def z_spot(t, half):
        early = t < 12
        step = jnp.where(early, sig * (1 + lax.div(t, 2)), -6 * sig)
        return piece(jnp.where(early, par, 1 - par), plane(step), half, lax.rem(t, 2))

    def h_spot(t, half):
        return piece(par, plane(-sig), half, 1 - t)

    def y_spot(t, half):
        n = lax.div(t, 2)
        k = jnp.where(n == 0, 0, jnp.where(n == 1, 7, n - 1))
        return piece(1 - par, plane(-sig * k), half, 1 - lax.rem(t, 2))

    def x_spot(r, t, half):
        by_z = lax.rem(t, 2) == r
        n = lax.div(t, 2)
        z_step = jnp.where(t < 12, sig * (1 + n), -6 * sig)
        y_step = jnp.where(t < 2, -sig, -sig * jnp.where(n == 1, 7, n - 1))
        z_par = jnp.where(t < 12, par, 1 - par)
        y_par = jnp.where(t < 2, par, 1 - par)
        return piece(jnp.where(by_z, z_par, y_par), plane(jnp.where(by_z, z_step, y_step)), half, r)

    def pass_over(ref, i):
        remote(ref, ref, c_send.at[i], c_recv.at[i], other).start()

    def arrived(ref, send, recv):
        remote(ref, ref, send, recv, other).wait_recv()

    def kv(ref_k, ref_v, which, g):
        cols = pl.ds(pl.multiple_of(g * 256, 256), 256)
        return (ref_k if which == 0 else ref_v).at[:, cols]

    def slot(buf, which, g):
        return buf.at[which, :, pl.ds(pl.multiple_of(g * 256, 256), 256)]

    def start_near(g):
        for which in range(2):
            remote(
                kv(k_hbm, v_hbm, which, g), slot(near, which, g),
                near_send.at[which, g], near_recv.at[which, g], y_near,
            ).start()

    start_near(0)
    for i in range(2):
        home = piece(par, z, mine, i)
        remote(source(mine, i), home, z_send.at[i], z_recv.at[i], z_out).start()
        home = piece(par, z, mine, 1 - i)
        remote(source(mine, 1 - i), home, h_send.at[i], h_recv.at[i], h_out).start()
        remote(source(mine, 1 - i), home, y_send.at[i], y_recv.at[i], y_far).start()

    @pl.loop(1, GROUPS)
    def _(g):
        start_near(g)

    loads = [
        pltpu.make_async_copy(q_hbm, q, in_sem.at[0]),
        pltpu.make_async_copy(k_hbm, own.at[0], in_sem.at[1]),
        pltpu.make_async_copy(v_hbm, own.at[1], in_sem.at[2]),
        pltpu.make_async_copy(
            w_hbm, weight.at[pl.ds(pl.multiple_of(SHARD * at, 16), SHARD), :], in_sem.at[3]
        ),
        pltpu.make_async_copy(stream_hbm, stream, in_sem.at[4]),
    ]
    for load in loads:
        load.start()
    for load in loads:
        load.wait()
    total[...] = stream[...].astype(jnp.float32)
    any_piece = weight.at[pl.ds(0, ROWS), pl.ds(0, COLS)]

    bias = jnp.where((z + par > 0) & (z + par < 8), 0.0, -1e30).astype(jnp.float32)
    ones = jnp.ones((BLOCK, HEAD_SIZE), jnp.bfloat16)

    def attend(h):
        cols = pl.ds(pl.multiple_of(h * HEAD_SIZE, HEAD_SIZE), HEAD_SIZE)
        query = q[:, cols]

        def score(buf):
            return lax.dot_general(
                query, buf[0, :, cols], (((1,), (1,)), ((), ())), preferred_element_type=jnp.float32
            )

        scores = [score(own), score(near), score(far) + bias]
        largest = jnp.maximum(jnp.maximum(scores[0], scores[1]), scores[2]).max(axis=1, keepdims=True)
        summed = None
        for buf, s in zip((own, near, far), scores):
            expon = jnp.exp2((s - largest) * SCALE).astype(jnp.bfloat16)
            values = jnp.concatenate([buf[1, :, cols], ones], axis=1)
            part = jnp.dot(expon, values, preferred_element_type=jnp.float32)
            summed = part if summed is None else summed + part
        ctx[:, cols] = (summed[:, :HEAD_SIZE] / summed[:, HEAD_SIZE:]).astype(jnp.bfloat16)

    def accumulate(row, depth):
        rows = pl.ds(pl.multiple_of(row, HEAD_SIZE), depth)

        @pl.loop(0, D // COLS)
        def _(n):
            cols = pl.ds(pl.multiple_of(n * COLS, COLS), COLS)
            total[:, cols] += jnp.dot(ctx[:, rows], weight[rows, cols], preferred_element_type=jnp.float32)

    def first_row(zz):
        return 640 * lax.div(zz, 2) + 384 * lax.rem(zz, 2)

    def due(zz):
        m = lax.rem(sig * (zz - z) + 16, 8)
        rows_here = jnp.where(m == 0, 4, jnp.where(m == 1, 6, jnp.where(m < 4, LAST, 14)))
        rows_here = jnp.where(m == 5, 12, jnp.where(m == 7, 8, rows_here))
        heads_here = jnp.where(zz < 4, jnp.where(zz < 2, 3 + 2 * zz, 5 + zz), jnp.where(zz < 5, 9, 7 + zz))
        return jnp.maximum(rows_here, heads_here)

    def project(t):
        @pl.loop(0, 4)
        def _(j):
            lower, upper = due(2 * j), due(2 * j + 1)

            @pl.when(lower == t)
            def _():
                accumulate(640 * j, 256)

            @pl.when(upper == t)
            def _():
                accumulate(640 * j + 384, 256)

            @pl.when(jnp.maximum(lower, upper) == t)
            def _():
                accumulate(640 * j + 256, 128)

    def handed(i):
        arrived(any_piece, c_send.at[i], c_recv.at[i])

    @pl.loop(0, LAST)
    def _(t):
        @pl.when(t < TICKS)
        def _():
            got = z_spot(t, mine)
            arrived(got, z_send.at[t], z_recv.at[t])

            @pl.when(t < 12)
            def _():
                k = jnp.where(t < 10, sig * (1 + lax.div(t, 2)), -7 * sig)
                ref = spot(jnp.where(t < 10, par, 1 - par), plane(k), lax.rem(t, 2))
                remote(ref, ref, z_send.at[t + 2], z_recv.at[t + 2], z_out).start()

            r = lax.rem(t, 2)

            @pl.when(t < 13)
            def _():
                remote(got, got, x_send.at[r, t], x_recv.at[r, t], x_dev(r)).start()

            pass_over(got, t)

            @pl.when(t < 2)
            def _():
                ref = h_spot(t, mine)
                arrived(ref, h_send.at[t], h_recv.at[t])
                remote(ref, ref, x_send.at[1 - r, t], x_recv.at[1 - r, t], x_dev(1 - r)).start()
                remote(ref, ref, y_send.at[t + 2], y_recv.at[t + 2], y_far).start()
                pass_over(ref, 14 + t)

            @pl.when((t > 0) & (t < 11))
            def _():
                ref = spot(par, plane(sig * (lax.div(t + 3, 2) - 1)), r)
                remote(ref, ref, y_send.at[t + 3], y_recv.at[t + 3], y_far).start()

            ref = y_spot(t, mine)
            arrived(ref, y_send.at[t], y_recv.at[t])

            @pl.when(t < 13)
            def _():
                i = jnp.where(t < 2, 13, t)
                remote(ref, ref, x_send.at[1 - r, i], x_recv.at[1 - r, i], x_dev(1 - r)).start()

            pass_over(ref, 16 + t)

        @pl.loop(lax.div(t * 25, 32), jnp.minimum(lax.div((t + 1) * 25, 32), GROUPS))
        def _(g):
            for which in range(2):
                ref = slot(near, which, g)
                arrived(ref, near_send.at[which, g], near_recv.at[which, g])
                remote(ref, slot(far, which, g), far_send.at[which, g], far_recv.at[which, g], h_out).start()

        @pl.when(t >= 2)
        def _():
            for r in range(2):
                ref = x_spot(r, t - 2, 1 - mine)
                arrived(ref, x_send.at[r, t - 2], x_recv.at[r, t - 2])
                pass_over(ref, 30 + r * 13 + t - 2)

        @pl.when(t == 3)
        def _():
            for r in range(2):
                ref = piece(1 - par, z, 1 - mine, r)
                arrived(ref, x_send.at[r, 13], x_recv.at[r, 13])
                pass_over(ref, 56 + r)

        @pl.when(t == 10)
        def _():
            ref = piece(par, plane(5 * sig), 1 - mine, 0)
            remote(ref, ref, d_send.at[0], d_recv.at[0], y_near).start()

        @pl.when(t == 13)
        def _():
            ref = piece(par, plane(6 * sig), 1 - mine, 1)
            remote(ref, ref, d_send.at[1], d_recv.at[1], y_near).start()

        def ready(s):
            return lax.div(jnp.maximum(s - 2, 0) * 25, 32)

        @pl.loop(ready(t), jnp.minimum(ready(t + 1), GROUPS))
        def _(g):
            for which in range(2):
                arrived(slot(far, which, g), far_send.at[which, g], far_recv.at[which, g])

            @pl.loop(0, 2)
            def _(i):
                attend(2 * g + i)

        @pl.when(t >= 1)
        def _():
            handed(t - 1)
            handed(16 + t - 1)

        @pl.when((t == 1) | (t == 2))
        def _():
            handed(14 + t - 1)

        @pl.when(t >= 3)
        def _():
            handed(30 + t - 3)
            handed(43 + t - 3)

        @pl.when(t == 4)
        def _():
            handed(56)
            handed(57)

        project(t)

    for i in range(2):
        ref = piece(1 - par, plane(-(5 + i) * sig), 1 - mine, i)
        arrived(ref, d_send.at[i], d_recv.at[i])
        pass_over(ref, 58 + i)

    for i in (42, 55, 58, 59):
        handed(i)

    @pl.loop(0, 4)
    def _(j):
        @pl.when(jnp.maximum(due(2 * j), due(2 * j + 1)) == LAST)
        def _():
            accumulate(640 * j + 256, 128)

    ends = [pl.ds(pl.multiple_of(first_row(plane(m * sig)), HEAD_SIZE), 256) for m in (2, 3)]

    @pl.loop(0, D // COLS)
    def _(n):
        cols = pl.ds(pl.multiple_of(n * COLS, COLS), COLS)
        product = total[:, cols]
        for rows in ends:
            product += jnp.dot(ctx[:, rows], weight[rows, cols], preferred_element_type=jnp.float32)
        out[:, cols] = product.astype(jnp.bfloat16)

    def sent(ref, send, recv):
        remote(ref, ref, send, recv, other).wait_send()

    @pl.loop(0, 14)
    def _(i):
        sent(any_piece, z_send.at[i], z_recv.at[i])
        sent(any_piece, y_send.at[i], y_recv.at[i])
        for r in range(2):
            sent(any_piece, x_send.at[r, i], x_recv.at[r, i])

    for i in range(2):
        sent(any_piece, h_send.at[i], h_recv.at[i])
        sent(any_piece, d_send.at[i], d_recv.at[i])

    @pl.loop(0, 60)
    def _(i):
        sent(any_piece, c_send.at[i], c_recv.at[i])

    @pl.loop(0, GROUPS)
    def _(g):
        for which in range(2):
            sent(slot(near, which, g), near_send.at[which, g], near_recv.at[which, g])
            sent(slot(far, which, g), far_send.at[which, g], far_recv.at[which, g])


def local(query_frames, key_frames, value_frames, stream, out_weight):
    dma = pltpu.SemaphoreType.DMA
    bf16 = jnp.bfloat16
    return pl.pallas_call(
        kernel,
        out_shape=jax.ShapeDtypeStruct((BLOCK, D), bf16),
        in_specs=[pl.BlockSpec(memory_space=pltpu.HBM)] * 5,
        out_specs=pl.BlockSpec(memory_space=pltpu.VMEM),
        scratch_shapes=[
            pltpu.VMEM((BLOCK, WIDTH), bf16),
            pltpu.VMEM((2, BLOCK, WIDTH), bf16),
            pltpu.VMEM((2, BLOCK, WIDTH), bf16),
            pltpu.VMEM((2, BLOCK, WIDTH), bf16),
            pltpu.VMEM((BLOCK, WIDTH), bf16),
            pltpu.VMEM((BLOCK, D), bf16),
            pltpu.VMEM((WIDTH, D), bf16),
            pltpu.VMEM((BLOCK, D), jnp.float32),
            dma((5,)),
            dma((14,)), dma((14,)),
            dma((2,)), dma((2,)),
            dma((14,)), dma((14,)),
            dma((2, 14)), dma((2, 14)),
            dma((2,)), dma((2,)),
            dma((60,)), dma((60,)),
            dma((2, GROUPS)), dma((2, GROUPS)),
            dma((2, GROUPS)), dma((2, GROUPS)),
        ],
        compiler_params=pltpu.CompilerParams(
            collective_id=0, has_side_effects=True, vmem_limit_bytes=50 * 1024 * 1024
        ),
    )(*[pltpu.with_memory_space_constraint(a, pltpu.HBM) for a in (query_frames, key_frames, value_frames, stream, out_weight)])


def solution(mesh):
    in_specs = (
        P(("dp", "ctx"), None),
        P(("dp", "ctx"), None),
        P(("dp", "ctx"), None),
        P(("dp", "ctx"), None),
        P("ctx", None),
    )
    out_specs = P(("dp", "ctx"), None)
    return jax.shard_map(local, mesh=mesh, in_specs=in_specs, out_specs=out_specs, check_vma=False)
```

```python
import jax
import jax.numpy as jnp
from jax import lax
from jax.experimental import pallas as pl
from jax.experimental.pallas import tpu as pltpu
from jax.sharding import PartitionSpec as P

HEADS = 20
HEAD_SIZE = 128
BLOCK = 256
WIDTH = 2560
D = 5120
SHARD = 160
ROWS = 80
COLS = 1280
GROUPS = 10
TICKS = 14
SCALE = HEAD_SIZE ** (-0.5) * 1.4426950408889634
MESH = pl.DeviceIdType.MESH


def kernel(
    q_hbm, k_hbm, v_hbm, stream_hbm, w_hbm, total,
    q, own, near, far, ctx, stream, weight,
    in_sem, z_send, z_recv, h_send, h_recv, y_send, y_recv, x_send, x_recv,
    d_send, d_recv, c_send, c_recv, near_send, near_recv, far_send, far_recv,
):
    dp = lax.axis_index("dp")
    at = lax.axis_index("ctx")
    core = lax.rem(dp, 2)
    x = lax.div(dp, 4)
    y_hi = lax.rem(lax.div(dp, 2), 2)
    z = lax.div(at, 2)
    par = lax.rem(at, 2)
    sig = 1 - 2 * par
    mine = lax.rem(x, 2)

    def plane(step):
        return lax.rem(z + step + 16, 8)

    z_out = (dp, plane(-sig) * 2 + par)
    h_out = (dp, plane(sig) * 2 + par)
    y_far = (dp + 2 - 4 * y_hi, at + 1 - 2 * par)
    y_near = (dp, at + 1 - 2 * par)
    other = (dp + 1 - 2 * core, at)

    def x_dev(r):
        return (lax.rem(dp + 4 + 8 * r, 16), at)

    barrier = pltpu.get_barrier_semaphore()
    for dev in (z_out, h_out, y_far, y_near, other, x_dev(0), x_dev(1)):
        pl.semaphore_signal(barrier, inc=1, device_id=dev, device_id_type=MESH)
    pl.semaphore_wait(barrier, 7)

    def piece(parity, zz, half, r):
        row = pl.multiple_of(SHARD * (2 * zz + parity) + ROWS * r, 16)
        col = pl.multiple_of(core * WIDTH + half * COLS, COLS)
        return weight.at[pl.ds(row, ROWS), pl.ds(col, COLS)]

    def source(half, r):
        row = pl.multiple_of(ROWS * r, 16)
        col = pl.multiple_of(core * WIDTH + half * COLS, COLS)
        return w_hbm.at[pl.ds(row, ROWS), pl.ds(col, COLS)]

    def remote(src, dst, send, recv, dev):
        return pltpu.make_async_remote_copy(
            src_ref=src, dst_ref=dst, send_sem=send, recv_sem=recv, device_id=dev, device_id_type=MESH
        )

    def spot(parity, zz, r):
        return piece(parity, zz, mine, r)

    def z_spot(t, half):
        early = t < 12
        step = jnp.where(early, sig * (1 + lax.div(t, 2)), -6 * sig)
        return piece(jnp.where(early, par, 1 - par), plane(step), half, lax.rem(t, 2))

    def h_spot(t, half):
        return piece(par, plane(-sig), half, 1 - t)

    def y_spot(t, half):
        n = lax.div(t, 2)
        k = jnp.where(n == 0, 0, jnp.where(n == 1, 7, n - 1))
        return piece(1 - par, plane(-sig * k), half, 1 - lax.rem(t, 2))

    def x_spot(r, t, half):
        by_z = lax.rem(t, 2) == r
        n = lax.div(t, 2)
        z_step = jnp.where(t < 12, sig * (1 + n), -6 * sig)
        y_step = jnp.where(t < 2, -sig, -sig * jnp.where(n == 1, 7, n - 1))
        z_par = jnp.where(t < 12, par, 1 - par)
        y_par = jnp.where(t < 2, par, 1 - par)
        return piece(jnp.where(by_z, z_par, y_par), plane(jnp.where(by_z, z_step, y_step)), half, r)

    def pass_over(ref, i):
        remote(ref, ref, c_send.at[i], c_recv.at[i], other).start()

    def arrived(ref, send, recv):
        remote(ref, ref, send, recv, other).wait_recv()

    def kv(ref_k, ref_v, which, g):
        cols = pl.ds(pl.multiple_of(g * 256, 256), 256)
        return (ref_k if which == 0 else ref_v).at[:, cols]

    def slot(buf, which, g):
        return buf.at[which, :, pl.ds(pl.multiple_of(g * 256, 256), 256)]

    def start_near(g):
        for which in range(2):
            remote(
                kv(k_hbm, v_hbm, which, g), slot(near, which, g),
                near_send.at[which, g], near_recv.at[which, g], y_near,
            ).start()

    start_near(0)
    for i in range(2):
        home = piece(par, z, mine, i)
        remote(source(mine, i), home, z_send.at[i], z_recv.at[i], z_out).start()
        home = piece(par, z, mine, 1 - i)
        remote(source(mine, 1 - i), home, h_send.at[i], h_recv.at[i], h_out).start()
        remote(source(mine, 1 - i), home, y_send.at[i], y_recv.at[i], y_far).start()

    @pl.loop(1, GROUPS)
    def _(g):
        start_near(g)

    loads = [
        pltpu.make_async_copy(q_hbm, q, in_sem.at[0]),
        pltpu.make_async_copy(k_hbm, own.at[0], in_sem.at[1]),
        pltpu.make_async_copy(v_hbm, own.at[1], in_sem.at[2]),
        pltpu.make_async_copy(
            w_hbm, weight.at[pl.ds(pl.multiple_of(SHARD * at, 16), SHARD), :], in_sem.at[3]
        ),
        pltpu.make_async_copy(stream_hbm, stream, in_sem.at[4]),
    ]
    for load in loads:
        load.start()
    for load in loads:
        load.wait()
    total[...] = stream[...].astype(jnp.float32)
    any_piece = weight.at[pl.ds(0, ROWS), pl.ds(0, COLS)]

    bias = jnp.where((z + par > 0) & (z + par < 8), 0.0, -1e30).astype(jnp.float32)
    ones = jnp.ones((BLOCK, HEAD_SIZE), jnp.bfloat16)

    def attend(h):
        cols = pl.ds(pl.multiple_of(h * HEAD_SIZE, HEAD_SIZE), HEAD_SIZE)
        query = q[:, cols]

        def score(buf):
            return lax.dot_general(
                query, buf[0, :, cols], (((1,), (1,)), ((), ())), preferred_element_type=jnp.float32
            )

        scores = [score(own), score(near), score(far) + bias]
        largest = jnp.maximum(jnp.maximum(scores[0], scores[1]), scores[2]).max(axis=1, keepdims=True)
        summed = None
        for buf, s in zip((own, near, far), scores):
            expon = jnp.exp2((s - largest) * SCALE).astype(jnp.bfloat16)
            values = jnp.concatenate([buf[1, :, cols], ones], axis=1)
            part = jnp.dot(expon, values, preferred_element_type=jnp.float32)
            summed = part if summed is None else summed + part
        ctx[:, cols] = (summed[:, :HEAD_SIZE] / summed[:, HEAD_SIZE:]).astype(jnp.bfloat16)

    def attend_group(g):
        for which in range(2):
            arrived(slot(far, which, g), far_send.at[which, g], far_recv.at[which, g])

        @pl.loop(0, 2)
        def _(i):
            attend(2 * g + i)

    def accumulate(row, depth):
        rows = pl.ds(pl.multiple_of(row, HEAD_SIZE), depth)

        @pl.loop(0, D // WIDTH)
        def _(n):
            cols = pl.ds(pl.multiple_of(n * WIDTH, WIDTH), WIDTH)
            total[:, cols] += jnp.dot(ctx[:, rows], weight[rows, cols], preferred_element_type=jnp.float32)

    def due(zz):
        m = lax.rem(sig * (zz - z) + 16, 8)
        rows_here = jnp.where(m == 0, 3, jnp.where(m == 1, 5, jnp.where(m < 4, TICKS, 13)))
        rows_here = jnp.where(m == 5, 11, jnp.where(m == 7, 7, rows_here))
        heads_here = jnp.where(zz < 4, jnp.where(zz < 1, 3, 5 + zz), jnp.where(zz < 5, 9, 7 + zz))
        return jnp.maximum(rows_here, heads_here)

    def project(t):
        @pl.loop(0, 4)
        def _(j):
            lower, upper = due(2 * j), due(2 * j + 1)

            @pl.when((lower == t) & (upper == t))
            def _():
                accumulate(640 * j, 640)

            @pl.when((lower == t) & (upper > t))
            def _():
                accumulate(640 * j, 256)

            @pl.when((lower == t) & (upper < t))
            def _():
                accumulate(640 * j, 384)

            @pl.when((upper == t) & (lower > t))
            def _():
                accumulate(640 * j + 384, 256)

            @pl.when((upper == t) & (lower < t))
            def _():
                accumulate(640 * j + 256, 384)

    def handed(i):
        arrived(any_piece, c_send.at[i], c_recv.at[i])

    @pl.loop(0, TICKS)
    def _(t):
        got = z_spot(t, mine)
        arrived(got, z_send.at[t], z_recv.at[t])

        @pl.when(t < 12)
        def _():
            k = jnp.where(t < 10, sig * (1 + lax.div(t, 2)), -7 * sig)
            ref = spot(jnp.where(t < 10, par, 1 - par), plane(k), lax.rem(t, 2))
            remote(ref, ref, z_send.at[t + 2], z_recv.at[t + 2], z_out).start()

        r = lax.rem(t, 2)

        @pl.when(t < 13)
        def _():
            remote(got, got, x_send.at[r, t], x_recv.at[r, t], x_dev(r)).start()

        pass_over(got, t)

        @pl.when(t < 2)
        def _():
            ref = h_spot(t, mine)
            arrived(ref, h_send.at[t], h_recv.at[t])
            remote(ref, ref, x_send.at[1 - r, t], x_recv.at[1 - r, t], x_dev(1 - r)).start()
            remote(ref, ref, y_send.at[t + 2], y_recv.at[t + 2], y_far).start()
            pass_over(ref, 14 + t)

        @pl.when((t > 0) & (t < 11))
        def _():
            ref = spot(par, plane(sig * (lax.div(t + 3, 2) - 1)), r)
            remote(ref, ref, y_send.at[t + 3], y_recv.at[t + 3], y_far).start()

        ref = y_spot(t, mine)
        arrived(ref, y_send.at[t], y_recv.at[t])

        @pl.when(t < 13)
        def _():
            i = jnp.where(t < 2, 13, t)
            remote(ref, ref, x_send.at[1 - r, i], x_recv.at[1 - r, i], x_dev(1 - r)).start()

        pass_over(ref, 16 + t)

        def pass_near(first, last):
            @pl.loop(first, jnp.minimum(last, GROUPS))
            def _(g):
                for which in range(2):
                    ref = slot(near, which, g)
                    arrived(ref, near_send.at[which, g], near_recv.at[which, g])
                    remote(
                        ref, slot(far, which, g), far_send.at[which, g], far_recv.at[which, g], h_out
                    ).start()

        def near_here(half):
            return lax.div(half * 25, 64)

        pass_near(near_here(2 * t + 1), near_here(2 * t + 2))

        def far_here(s):
            return lax.div(jnp.maximum((s - 1) * 25 - 8, 0), 32)

        @pl.loop(far_here(t - 1), far_here(t))
        def _(g):
            attend_group(g)

        @pl.when(t >= 1)
        def _():
            for r in range(2):
                ref = x_spot(r, t - 1, 1 - mine)
                arrived(ref, x_send.at[r, t - 1], x_recv.at[r, t - 1])
                pass_over(ref, 30 + r * 13 + t - 1)

        @pl.when(t == 2)
        def _():
            for r in range(2):
                ref = piece(1 - par, z, 1 - mine, r)
                arrived(ref, x_send.at[r, 13], x_recv.at[r, 13])
                pass_over(ref, 56 + r)

        @pl.when(t == 9)
        def _():
            ref = piece(par, plane(5 * sig), 1 - mine, 0)
            remote(ref, ref, d_send.at[0], d_recv.at[0], y_near).start()

        @pl.when(t == 12)
        def _():
            ref = piece(par, plane(6 * sig), 1 - mine, 1)
            remote(ref, ref, d_send.at[1], d_recv.at[1], y_near).start()

        pass_near(near_here(2 * t + 2), near_here(2 * t + 3))

        @pl.when(t >= 1)
        def _():
            handed(t - 1)
            handed(16 + t - 1)

        @pl.when((t == 1) | (t == 2))
        def _():
            handed(14 + t - 1)

        @pl.when(t >= 2)
        def _():
            handed(30 + t - 2)
            handed(43 + t - 2)

        @pl.when(t == 3)
        def _():
            handed(56)
            handed(57)

        project(t)

    for i in range(2):
        ref = piece(1 - par, plane(-(5 + i) * sig), 1 - mine, i)
        arrived(ref, d_send.at[i], d_recv.at[i])
        pass_over(ref, 58 + i)

    attend_group(GROUPS - 1)

    for i in (13, 29, 42, 55, 58, 59):
        handed(i)

    project(TICKS)

    def sent(ref, send, recv):
        remote(ref, ref, send, recv, other).wait_send()

    @pl.loop(0, 14)
    def _(i):
        sent(any_piece, z_send.at[i], z_recv.at[i])
        sent(any_piece, y_send.at[i], y_recv.at[i])
        for r in range(2):
            sent(any_piece, x_send.at[r, i], x_recv.at[r, i])

    for i in range(2):
        sent(any_piece, h_send.at[i], h_recv.at[i])
        sent(any_piece, d_send.at[i], d_recv.at[i])

    @pl.loop(0, 60)
    def _(i):
        sent(any_piece, c_send.at[i], c_recv.at[i])

    @pl.loop(0, GROUPS)
    def _(g):
        for which in range(2):
            sent(slot(near, which, g), near_send.at[which, g], near_recv.at[which, g])
            sent(slot(far, which, g), far_send.at[which, g], far_recv.at[which, g])


def local(query_frames, key_frames, value_frames, stream, out_weight):
    dma = pltpu.SemaphoreType.DMA
    bf16 = jnp.bfloat16
    total = pl.pallas_call(
        kernel,
        out_shape=jax.ShapeDtypeStruct((BLOCK, D), jnp.float32),
        in_specs=[pl.BlockSpec(memory_space=pltpu.HBM)] * 5,
        out_specs=pl.BlockSpec(memory_space=pltpu.VMEM),
        scratch_shapes=[
            pltpu.VMEM((BLOCK, WIDTH), bf16),
            pltpu.VMEM((2, BLOCK, WIDTH), bf16),
            pltpu.VMEM((2, BLOCK, WIDTH), bf16),
            pltpu.VMEM((2, BLOCK, WIDTH), bf16),
            pltpu.VMEM((BLOCK, WIDTH), bf16),
            pltpu.VMEM((BLOCK, D), bf16),
            pltpu.VMEM((WIDTH, D), bf16),
            dma((5,)),
            dma((14,)), dma((14,)),
            dma((2,)), dma((2,)),
            dma((14,)), dma((14,)),
            dma((2, 14)), dma((2, 14)),
            dma((2,)), dma((2,)),
            dma((60,)), dma((60,)),
            dma((2, GROUPS)), dma((2, GROUPS)),
            dma((2, GROUPS)), dma((2, GROUPS)),
        ],
        compiler_params=pltpu.CompilerParams(
            collective_id=0, has_side_effects=True, vmem_limit_bytes=44 * 1024 * 1024
        ),
    )(*[pltpu.with_memory_space_constraint(a, pltpu.HBM) for a in (query_frames, key_frames, value_frames, stream, out_weight)])
    return total.astype(bf16)


def solution(mesh):
    in_specs = (
        P(("dp", "ctx"), None),
        P(("dp", "ctx"), None),
        P(("dp", "ctx"), None),
        P(("dp", "ctx"), None),
        P("ctx", None),
    )
    out_specs = P(("dp", "ctx"), None)
    return jax.shard_map(local, mesh=mesh, in_specs=in_specs, out_specs=out_specs, check_vma=False)
```

```python
import jax
import jax.numpy as jnp
from jax import lax
from jax.experimental import pallas as pl
from jax.experimental.pallas import tpu as pltpu
from jax.sharding import PartitionSpec as P

HEADS = 20
HEAD_SIZE = 128
BLOCK = 256
WIDTH = 2560
D = 5120
SHARD = 160
ROWS = 80
COLS = 1280
GROUPS = 10
TICKS = 14
SCALE = HEAD_SIZE ** (-0.5) * 1.4426950408889634
MESH = pl.DeviceIdType.MESH


def kernel(
    q_hbm, k_hbm, v_hbm, stream_hbm, w_hbm, total,
    q, own, near, far, ctx, stream, weight,
    in_sem, z_send, z_recv, h_send, h_recv, y_send, y_recv, x_send, x_recv,
    d_send, d_recv, c_send, c_recv, near_send, near_recv, far_send, far_recv,
):
    dp = lax.axis_index("dp")
    at = lax.axis_index("ctx")
    core = lax.rem(dp, 2)
    x = lax.div(dp, 4)
    y_hi = lax.rem(lax.div(dp, 2), 2)
    z = lax.div(at, 2)
    par = lax.rem(at, 2)
    sig = 1 - 2 * par
    mine = lax.rem(x, 2)

    def plane(step):
        return lax.rem(z + step + 16, 8)

    z_out = (dp, plane(-sig) * 2 + par)
    h_out = (dp, plane(sig) * 2 + par)
    y_far = (dp + 2 - 4 * y_hi, at + 1 - 2 * par)
    y_near = (dp, at + 1 - 2 * par)
    other = (dp + 1 - 2 * core, at)

    def x_dev(r):
        return (lax.rem(dp + 4 + 8 * r, 16), at)

    barrier = pltpu.get_barrier_semaphore()
    for dev in (z_out, h_out, y_far, y_near, other, x_dev(0), x_dev(1)):
        pl.semaphore_signal(barrier, inc=1, device_id=dev, device_id_type=MESH)
    pl.semaphore_wait(barrier, 7)

    def piece(parity, zz, half, r):
        row = pl.multiple_of(SHARD * (2 * zz + parity) + ROWS * r, 16)
        col = pl.multiple_of(core * WIDTH + half * COLS, COLS)
        return weight.at[pl.ds(row, ROWS), pl.ds(col, COLS)]

    def source(half, r):
        row = pl.multiple_of(ROWS * r, 16)
        col = pl.multiple_of(core * WIDTH + half * COLS, COLS)
        return w_hbm.at[pl.ds(row, ROWS), pl.ds(col, COLS)]

    def remote(src, dst, send, recv, dev):
        return pltpu.make_async_remote_copy(
            src_ref=src, dst_ref=dst, send_sem=send, recv_sem=recv, device_id=dev, device_id_type=MESH
        )

    def spot(parity, zz, r):
        return piece(parity, zz, mine, r)

    def z_spot(t, half):
        early = t < 12
        step = jnp.where(early, sig * (1 + lax.div(t, 2)), -6 * sig)
        return piece(jnp.where(early, par, 1 - par), plane(step), half, lax.rem(t, 2))

    def h_spot(t, half):
        return piece(par, plane(-sig), half, 1 - t)

    def y_spot(t, half):
        n = lax.div(t, 2)
        k = jnp.where(n == 0, 0, jnp.where(n == 1, 7, n - 1))
        return piece(1 - par, plane(-sig * k), half, 1 - lax.rem(t, 2))

    def x_spot(r, t, half):
        by_z = lax.rem(t, 2) == r
        n = lax.div(t, 2)
        z_step = jnp.where(t < 12, sig * (1 + n), -6 * sig)
        y_step = jnp.where(t < 2, -sig, -sig * jnp.where(n == 1, 7, n - 1))
        z_par = jnp.where(t < 12, par, 1 - par)
        y_par = jnp.where(t < 2, par, 1 - par)
        return piece(jnp.where(by_z, z_par, y_par), plane(jnp.where(by_z, z_step, y_step)), half, r)

    def pass_over(ref, i):
        remote(ref, ref, c_send.at[i], c_recv.at[i], other).start()

    def arrived(ref, send, recv):
        remote(ref, ref, send, recv, other).wait_recv()

    def kv(ref_k, ref_v, which, g):
        cols = pl.ds(pl.multiple_of(g * 256, 256), 256)
        return (ref_k if which == 0 else ref_v).at[:, cols]

    def slot(buf, which, g):
        return buf.at[which, :, pl.ds(pl.multiple_of(g * 256, 256), 256)]

    def start_near(g):
        for which in range(2):
            remote(
                kv(k_hbm, v_hbm, which, g), slot(near, which, g),
                near_send.at[which, g], near_recv.at[which, g], y_near,
            ).start()

    start_near(0)
    for i in range(2):
        home = piece(par, z, mine, i)
        remote(source(mine, i), home, z_send.at[i], z_recv.at[i], z_out).start()
        home = piece(par, z, mine, 1 - i)
        remote(source(mine, 1 - i), home, h_send.at[i], h_recv.at[i], h_out).start()
        remote(source(mine, 1 - i), home, y_send.at[i], y_recv.at[i], y_far).start()

    @pl.loop(1, GROUPS)
    def _(g):
        start_near(g)

    loads = [
        pltpu.make_async_copy(q_hbm, q, in_sem.at[0]),
        pltpu.make_async_copy(k_hbm, own.at[0], in_sem.at[1]),
        pltpu.make_async_copy(v_hbm, own.at[1], in_sem.at[2]),
        pltpu.make_async_copy(
            w_hbm, weight.at[pl.ds(pl.multiple_of(SHARD * at, 16), SHARD), :], in_sem.at[3]
        ),
        pltpu.make_async_copy(stream_hbm, stream, in_sem.at[4]),
    ]
    for load in loads:
        load.start()
    for load in loads:
        load.wait()
    total[...] = stream[...].astype(jnp.float32)
    any_piece = weight.at[pl.ds(0, ROWS), pl.ds(0, COLS)]

    bias = jnp.where((z + par > 0) & (z + par < 8), 0.0, -1e30).astype(jnp.float32)
    ones = jnp.ones((BLOCK, HEAD_SIZE), jnp.bfloat16)

    def attend(h):
        cols = pl.ds(pl.multiple_of(h * HEAD_SIZE, HEAD_SIZE), HEAD_SIZE)
        query = q[:, cols]

        def score(buf):
            return lax.dot_general(
                query, buf[0, :, cols], (((1,), (1,)), ((), ())), preferred_element_type=jnp.float32
            )

        scores = [score(own), score(near), score(far) + bias]
        largest = jnp.maximum(jnp.maximum(scores[0], scores[1]), scores[2]).max(axis=1, keepdims=True)
        summed = None
        for buf, s in zip((own, near, far), scores):
            expon = jnp.exp2((s - largest) * SCALE).astype(jnp.bfloat16)
            values = jnp.concatenate([buf[1, :, cols], ones], axis=1)
            part = jnp.dot(expon, values, preferred_element_type=jnp.float32)
            summed = part if summed is None else summed + part
        ctx[:, cols] = (summed[:, :HEAD_SIZE] / summed[:, HEAD_SIZE:]).astype(jnp.bfloat16)

    def attend_group(g):
        for which in range(2):
            arrived(slot(far, which, g), far_send.at[which, g], far_recv.at[which, g])

        @pl.loop(0, 2)
        def _(i):
            attend(2 * g + i)

    def accumulate(row, depth):
        rows = pl.ds(pl.multiple_of(row, HEAD_SIZE), depth)

        total[...] += jnp.dot(ctx[:, rows], weight[rows, :], preferred_element_type=jnp.float32)

    def due(zz):
        m = lax.rem(sig * (zz - z) + 16, 8)
        rows_here = jnp.where(m == 0, 3, jnp.where(m == 1, 5, jnp.where(m < 4, TICKS, 13)))
        rows_here = jnp.where(m == 5, 11, jnp.where(m == 7, 7, rows_here))
        heads_here = jnp.where(zz < 4, jnp.where(zz < 1, 3, 5 + zz), jnp.where(zz < 5, 9, 7 + zz))
        return jnp.maximum(rows_here, heads_here)

    def project(t):
        @pl.loop(0, 4)
        def _(j):
            lower, upper = due(2 * j), due(2 * j + 1)

            @pl.when((lower == t) & (upper == t))
            def _():
                accumulate(640 * j, 640)

            @pl.when((lower == t) & (upper > t))
            def _():
                accumulate(640 * j, 256)

            @pl.when((lower == t) & (upper < t))
            def _():
                accumulate(640 * j, 384)

            @pl.when((upper == t) & (lower > t))
            def _():
                accumulate(640 * j + 384, 256)

            @pl.when((upper == t) & (lower < t))
            def _():
                accumulate(640 * j + 256, 384)

    def handed(i):
        arrived(any_piece, c_send.at[i], c_recv.at[i])

    @pl.loop(0, TICKS)
    def _(t):
        got = z_spot(t, mine)
        arrived(got, z_send.at[t], z_recv.at[t])

        @pl.when(t < 12)
        def _():
            k = jnp.where(t < 10, sig * (1 + lax.div(t, 2)), -7 * sig)
            ref = spot(jnp.where(t < 10, par, 1 - par), plane(k), lax.rem(t, 2))
            remote(ref, ref, z_send.at[t + 2], z_recv.at[t + 2], z_out).start()

        r = lax.rem(t, 2)

        @pl.when(t < 12)
        def _():
            remote(got, got, x_send.at[r, t], x_recv.at[r, t], x_dev(r)).start()

        pass_over(got, t)

        @pl.when(t < 2)
        def _():
            ref = h_spot(t, mine)
            arrived(ref, h_send.at[t], h_recv.at[t])
            remote(ref, ref, x_send.at[1 - r, t], x_recv.at[1 - r, t], x_dev(1 - r)).start()
            remote(ref, ref, y_send.at[t + 2], y_recv.at[t + 2], y_far).start()
            pass_over(ref, 15 + t)

        @pl.when((t > 0) & (t < 11))
        def _():
            ref = spot(par, plane(sig * (lax.div(t + 3, 2) - 1)), r)
            remote(ref, ref, y_send.at[t + 3], y_recv.at[t + 3], y_far).start()

        ref = y_spot(t, mine)
        arrived(ref, y_send.at[t], y_recv.at[t])

        @pl.when(t < 12)
        def _():
            i = jnp.where(t < 2, 12, t)
            remote(ref, ref, x_send.at[1 - r, i], x_recv.at[1 - r, i], x_dev(1 - r)).start()

        pass_over(ref, 17 + t)

        @pl.when(t >= 2)
        def _():
            for side in range(2):
                ref = x_spot(side, t - 2, 1 - mine)
                arrived(ref, x_send.at[side, t - 2], x_recv.at[side, t - 2])
                pass_over(ref, 32 + side * 12 + t - 2)

        @pl.when(t == 3)
        def _():
            for side in range(2):
                ref = piece(1 - par, z, 1 - mine, side)
                arrived(ref, x_send.at[side, 12], x_recv.at[side, 12])
                pass_over(ref, 56 + side)

        @pl.when(t == 11)
        def _():
            ref = piece(par, plane(5 * sig), 1 - mine, 0)
            remote(ref, ref, y_send.at[14], y_recv.at[14], y_far).start()
            ref = piece(par, plane(5 * sig), 1 - mine, 1)
            remote(ref, ref, d_send.at[0], d_recv.at[0], y_near).start()

        @pl.when(t == 12)
        def _():
            ref = piece(1 - par, plane(-7 * sig), 1 - mine, 1)
            remote(ref, ref, z_send.at[14], z_recv.at[14], z_out).start()
            ref = piece(par, plane(6 * sig), 1 - mine, 0)
            remote(ref, ref, d_send.at[1], d_recv.at[1], y_near).start()

        def pass_near(first, last):
            @pl.loop(first, jnp.minimum(last, GROUPS))
            def _(g):
                for which in range(2):
                    ref = slot(near, which, g)
                    arrived(ref, near_send.at[which, g], near_recv.at[which, g])
                    remote(
                        ref, slot(far, which, g), far_send.at[which, g], far_recv.at[which, g], h_out
                    ).start()

        def near_here(half):
            return lax.div(half * 25, 64)

        pass_near(near_here(2 * t + 1), near_here(2 * t + 2))

        def far_here(s):
            return lax.div(jnp.maximum((s - 1) * 25 - 8, 0), 32)

        @pl.loop(far_here(t - 1), far_here(t))
        def _(g):
            attend_group(g)

        pass_near(near_here(2 * t + 2), near_here(2 * t + 3))

        @pl.when(t >= 1)
        def _():
            handed(t - 1)
            handed(17 + t - 1)

        @pl.when((t == 1) | (t == 2))
        def _():
            handed(15 + t - 1)

        @pl.when(t >= 2)
        def _():
            handed(32 + t - 2)
            handed(44 + t - 2)

        @pl.when(t == 3)
        def _():
            handed(56)
            handed(57)

        project(t)

    def last(send, recv, step, r, i):
        ref = piece(1 - par, plane(-step * sig), 1 - mine, r)
        arrived(ref, send, recv)
        pass_over(ref, i)

    last(d_send.at[0], d_recv.at[0], 5, 1, 58)
    last(d_send.at[1], d_recv.at[1], 6, 0, 59)
    last(y_send.at[14], y_recv.at[14], 5, 0, 31)
    last(z_send.at[14], z_recv.at[14], 6, 1, 14)
    attend_group(GROUPS - 1)

    for i in (13, 30, 14, 31, 58, 59):
        handed(i)

    project(TICKS)

    def sent(ref, send, recv):
        remote(ref, ref, send, recv, other).wait_send()

    @pl.loop(0, 15)
    def _(i):
        sent(any_piece, z_send.at[i], z_recv.at[i])
        sent(any_piece, y_send.at[i], y_recv.at[i])

    @pl.loop(0, 13)
    def _(i):
        for r in range(2):
            sent(any_piece, x_send.at[r, i], x_recv.at[r, i])

    for i in range(2):
        sent(any_piece, h_send.at[i], h_recv.at[i])
        sent(any_piece, d_send.at[i], d_recv.at[i])

    @pl.loop(0, 60)
    def _(i):
        sent(any_piece, c_send.at[i], c_recv.at[i])

    @pl.loop(0, GROUPS)
    def _(g):
        for which in range(2):
            sent(slot(near, which, g), near_send.at[which, g], near_recv.at[which, g])
            sent(slot(far, which, g), far_send.at[which, g], far_recv.at[which, g])


def local(query_frames, key_frames, value_frames, stream, out_weight):
    dma = pltpu.SemaphoreType.DMA
    bf16 = jnp.bfloat16
    total = pl.pallas_call(
        kernel,
        out_shape=jax.ShapeDtypeStruct((BLOCK, D), jnp.float32),
        in_specs=[pl.BlockSpec(memory_space=pltpu.HBM)] * 5,
        out_specs=pl.BlockSpec(memory_space=pltpu.VMEM),
        scratch_shapes=[
            pltpu.VMEM((BLOCK, WIDTH), bf16),
            pltpu.VMEM((2, BLOCK, WIDTH), bf16),
            pltpu.VMEM((2, BLOCK, WIDTH), bf16),
            pltpu.VMEM((2, BLOCK, WIDTH), bf16),
            pltpu.VMEM((BLOCK, WIDTH), bf16),
            pltpu.VMEM((BLOCK, D), bf16),
            pltpu.VMEM((WIDTH, D), bf16),
            dma((5,)),
            dma((15,)), dma((15,)),
            dma((2,)), dma((2,)),
            dma((15,)), dma((15,)),
            dma((2, 13)), dma((2, 13)),
            dma((2,)), dma((2,)),
            dma((60,)), dma((60,)),
            dma((2, GROUPS)), dma((2, GROUPS)),
            dma((2, GROUPS)), dma((2, GROUPS)),
        ],
        compiler_params=pltpu.CompilerParams(
            collective_id=0, has_side_effects=True, vmem_limit_bytes=44 * 1024 * 1024
        ),
    )(*[pltpu.with_memory_space_constraint(a, pltpu.HBM) for a in (query_frames, key_frames, value_frames, stream, out_weight)])
    return total.astype(bf16)


def solution(mesh):
    in_specs = (
        P(("dp", "ctx"), None),
        P(("dp", "ctx"), None),
        P(("dp", "ctx"), None),
        P(("dp", "ctx"), None),
        P("ctx", None),
    )
    out_specs = P(("dp", "ctx"), None)
    return jax.shard_map(local, mesh=mesh, in_specs=in_specs, out_specs=out_specs, check_vma=False)
```

```python
import jax
import jax.numpy as jnp
from jax import lax
from jax.experimental import pallas as pl
from jax.experimental.pallas import tpu as pltpu
from jax.sharding import PartitionSpec as P

HEADS = 20
HEAD_SIZE = 128
BLOCK = 256
WIDTH = 2560
D = 5120
SHARD = 160
ROWS = 80
COLS = 1280
GROUPS = 10
TICKS = 14
SCALE = HEAD_SIZE ** (-0.5) * 1.4426950408889634
MESH = pl.DeviceIdType.MESH


def kernel(
    q_hbm, k_hbm, v_hbm, stream_hbm, w_hbm, total,
    q, own, near, far, ctx, stream, weight,
    in_sem, z_send, z_recv, h_send, h_recv, y_send, y_recv, x_send, x_recv,
    d_send, d_recv, c_send, c_recv, near_send, near_recv, far_send, far_recv,
):
    dp = lax.axis_index("dp")
    at = lax.axis_index("ctx")
    core = lax.rem(dp, 2)
    x = lax.div(dp, 4)
    y_hi = lax.rem(lax.div(dp, 2), 2)
    z = lax.div(at, 2)
    par = lax.rem(at, 2)
    sig = 1 - 2 * par
    mine = lax.rem(x, 2)

    def plane(step):
        return lax.rem(z + step + 16, 8)

    z_out = (dp, plane(-sig) * 2 + par)
    h_out = (dp, plane(sig) * 2 + par)
    y_far = (dp + 2 - 4 * y_hi, at + 1 - 2 * par)
    y_near = (dp, at + 1 - 2 * par)
    other = (dp + 1 - 2 * core, at)

    def x_dev(r):
        return (lax.rem(dp + 4 + 8 * r, 16), at)

    barrier = pltpu.get_barrier_semaphore()
    for dev in (z_out, h_out, y_far, y_near, other, x_dev(0), x_dev(1)):
        pl.semaphore_signal(barrier, inc=1, device_id=dev, device_id_type=MESH)
    pl.semaphore_wait(barrier, 7)

    def piece(parity, zz, half, r):
        row = pl.multiple_of(SHARD * (2 * zz + parity) + ROWS * r, 16)
        col = pl.multiple_of(core * WIDTH + half * COLS, COLS)
        return weight.at[pl.ds(row, ROWS), pl.ds(col, COLS)]

    def source(half, r):
        row = pl.multiple_of(ROWS * r, 16)
        col = pl.multiple_of(core * WIDTH + half * COLS, COLS)
        return w_hbm.at[pl.ds(row, ROWS), pl.ds(col, COLS)]

    def remote(src, dst, send, recv, dev):
        return pltpu.make_async_remote_copy(
            src_ref=src, dst_ref=dst, send_sem=send, recv_sem=recv, device_id=dev, device_id_type=MESH
        )

    def spot(parity, zz, r):
        return piece(parity, zz, mine, r)

    def z_spot(t, half):
        early = t < 12
        step = jnp.where(early, sig * (1 + lax.div(t, 2)), -6 * sig)
        return piece(jnp.where(early, par, 1 - par), plane(step), half, lax.rem(t, 2))

    def h_spot(t, half):
        return piece(par, plane(-sig), half, 1 - t)

    def y_spot(t, half):
        n = lax.div(t, 2)
        k = jnp.where(n == 0, 0, jnp.where(n == 1, 7, n - 1))
        return piece(1 - par, plane(-sig * k), half, 1 - lax.rem(t, 2))

    def x_spot(r, t, half):
        by_z = lax.rem(t, 2) == r
        n = lax.div(t, 2)
        z_step = jnp.where(t < 12, sig * (1 + n), -6 * sig)
        y_step = jnp.where(t < 2, -sig, -sig * jnp.where(n == 1, 7, n - 1))
        z_par = jnp.where(t < 12, par, 1 - par)
        y_par = jnp.where(t < 2, par, 1 - par)
        return piece(jnp.where(by_z, z_par, y_par), plane(jnp.where(by_z, z_step, y_step)), half, r)

    def pass_over(ref, i):
        remote(ref, ref, c_send.at[i], c_recv.at[i], other).start()

    def arrived(ref, send, recv):
        remote(ref, ref, send, recv, other).wait_recv()

    def kv(ref_k, ref_v, which, g):
        cols = pl.ds(pl.multiple_of(g * 256, 256), 256)
        return (ref_k if which == 0 else ref_v).at[:, cols]

    def slot(buf, which, g):
        return buf.at[which, :, pl.ds(pl.multiple_of(g * 256, 256), 256)]

    def start_near(g):
        for which in range(2):
            remote(
                kv(k_hbm, v_hbm, which, g), slot(near, which, g),
                near_send.at[which, g], near_recv.at[which, g], y_near,
            ).start()

    start_near(0)
    for i in range(2):
        home = piece(par, z, mine, i)
        remote(source(mine, i), home, z_send.at[i], z_recv.at[i], z_out).start()
        home = piece(par, z, mine, 1 - i)
        remote(source(mine, 1 - i), home, h_send.at[i], h_recv.at[i], h_out).start()
        remote(source(mine, 1 - i), home, y_send.at[i], y_recv.at[i], y_far).start()

    @pl.loop(1, GROUPS)
    def _(g):
        start_near(g)

    loads = [
        pltpu.make_async_copy(q_hbm, q, in_sem.at[0]),
        pltpu.make_async_copy(k_hbm, own.at[0], in_sem.at[1]),
        pltpu.make_async_copy(v_hbm, own.at[1], in_sem.at[2]),
        pltpu.make_async_copy(
            w_hbm, weight.at[pl.ds(pl.multiple_of(SHARD * at, 16), SHARD), :], in_sem.at[3]
        ),
        pltpu.make_async_copy(stream_hbm, stream, in_sem.at[4]),
    ]
    for load in loads:
        load.start()
    for load in loads:
        load.wait()
    total[...] = stream[...].astype(jnp.float32)
    any_piece = weight.at[pl.ds(0, ROWS), pl.ds(0, COLS)]

    bias = jnp.where((z + par > 0) & (z + par < 8), 0.0, -1e30).astype(jnp.float32)
    ones = jnp.ones((BLOCK, HEAD_SIZE), jnp.bfloat16)

    def attend(h):
        cols = pl.ds(pl.multiple_of(h * HEAD_SIZE, HEAD_SIZE), HEAD_SIZE)
        query = q[:, cols]

        def score(buf):
            return lax.dot_general(
                query, buf[0, :, cols], (((1,), (1,)), ((), ())), preferred_element_type=jnp.float32
            )

        scores = [score(own), score(near), score(far) + bias]
        largest = jnp.maximum(jnp.maximum(scores[0], scores[1]), scores[2]).max(axis=1, keepdims=True)
        summed = None
        for buf, s in zip((own, near, far), scores):
            expon = jnp.exp2((s - largest) * SCALE).astype(jnp.bfloat16)
            values = jnp.concatenate([buf[1, :, cols], ones], axis=1)
            part = jnp.dot(expon, values, preferred_element_type=jnp.float32)
            summed = part if summed is None else summed + part
        ctx[:, cols] = (summed[:, :HEAD_SIZE] / summed[:, HEAD_SIZE:]).astype(jnp.bfloat16)

    def attend_group(g):
        for which in range(2):
            arrived(slot(far, which, g), far_send.at[which, g], far_recv.at[which, g])

        @pl.loop(0, 2)
        def _(i):
            attend(2 * g + i)

    def accumulate(row, depth):
        rows = pl.ds(pl.multiple_of(row, HEAD_SIZE), depth)

        total[...] += jnp.dot(ctx[:, rows], weight[rows, :], preferred_element_type=jnp.float32)

    def due(zz):
        m = lax.rem(sig * (zz - z) + 16, 8)
        rows_here = jnp.where(m == 0, 3, jnp.where(m == 1, 5, jnp.where(m < 4, TICKS, 13)))
        rows_here = jnp.where(m == 5, 11, jnp.where(m == 7, 7, rows_here))
        heads_here = jnp.where(zz < 4, jnp.where(zz < 1, 3, 5 + zz), jnp.where(zz < 5, 9, 7 + zz))
        return jnp.maximum(rows_here, heads_here)

    def project(t):
        @pl.loop(0, 4)
        def _(j):
            lower, upper = due(2 * j), due(2 * j + 1)

            @pl.when((lower == t) & (upper == t))
            def _():
                accumulate(640 * j, 640)

            @pl.when((lower == t) & (upper > t))
            def _():
                accumulate(640 * j, 256)

            @pl.when((lower == t) & (upper < t))
            def _():
                accumulate(640 * j, 384)

            @pl.when((upper == t) & (lower > t))
            def _():
                accumulate(640 * j + 384, 256)

            @pl.when((upper == t) & (lower < t))
            def _():
                accumulate(640 * j + 256, 384)

    def handed(i):
        arrived(any_piece, c_send.at[i], c_recv.at[i])

    @pl.loop(0, TICKS)
    def _(t):
        got = z_spot(t, mine)
        arrived(got, z_send.at[t], z_recv.at[t])

        @pl.when(t < 12)
        def _():
            k = jnp.where(t < 10, sig * (1 + lax.div(t, 2)), -7 * sig)
            ref = spot(jnp.where(t < 10, par, 1 - par), plane(k), lax.rem(t, 2))
            remote(ref, ref, z_send.at[t + 2], z_recv.at[t + 2], z_out).start()

        r = lax.rem(t, 2)

        @pl.when(t < 12)
        def _():
            remote(got, got, x_send.at[r, t], x_recv.at[r, t], x_dev(r)).start()

        pass_over(got, t)

        @pl.when(t < 2)
        def _():
            ref = h_spot(t, mine)
            arrived(ref, h_send.at[t], h_recv.at[t])
            remote(ref, ref, x_send.at[1 - r, t], x_recv.at[1 - r, t], x_dev(1 - r)).start()
            remote(ref, ref, y_send.at[t + 2], y_recv.at[t + 2], y_far).start()
            pass_over(ref, 15 + t)

        @pl.when((t > 0) & (t < 11))
        def _():
            ref = spot(par, plane(sig * (lax.div(t + 3, 2) - 1)), r)
            remote(ref, ref, y_send.at[t + 3], y_recv.at[t + 3], y_far).start()

        ref = y_spot(t, mine)
        arrived(ref, y_send.at[t], y_recv.at[t])

        @pl.when(t < 12)
        def _():
            i = jnp.where(t < 2, 12, t)
            remote(ref, ref, x_send.at[1 - r, i], x_recv.at[1 - r, i], x_dev(1 - r)).start()

        pass_over(ref, 17 + t)

        def pass_near(first, last):
            @pl.loop(first, jnp.minimum(last, GROUPS))
            def _(g):
                for which in range(2):
                    ref = slot(near, which, g)
                    arrived(ref, near_send.at[which, g], near_recv.at[which, g])
                    remote(
                        ref, slot(far, which, g), far_send.at[which, g], far_recv.at[which, g], h_out
                    ).start()

        def near_here(half):
            return lax.div(half * 25, 64)

        pass_near(near_here(2 * t + 1), near_here(2 * t + 2))

        def far_here(s):
            return lax.div(jnp.maximum((s - 1) * 25 - 8, 0), 32)

        @pl.loop(far_here(t - 1), far_here(t))
        def _(g):
            attend_group(g)

        @pl.when(t >= 2)
        def _():
            for side in range(2):
                ref = x_spot(side, t - 2, 1 - mine)
                arrived(ref, x_send.at[side, t - 2], x_recv.at[side, t - 2])
                pass_over(ref, 32 + side * 12 + t - 2)

        @pl.when(t == 3)
        def _():
            for side in range(2):
                ref = piece(1 - par, z, 1 - mine, side)
                arrived(ref, x_send.at[side, 12], x_recv.at[side, 12])
                pass_over(ref, 56 + side)

        @pl.when(t == 11)
        def _():
            ref = piece(par, plane(5 * sig), 1 - mine, 0)
            remote(ref, ref, y_send.at[14], y_recv.at[14], y_far).start()
            ref = piece(par, plane(5 * sig), 1 - mine, 1)
            remote(ref, ref, d_send.at[0], d_recv.at[0], y_near).start()

        @pl.when(t == 12)
        def _():
            ref = piece(1 - par, plane(-7 * sig), 1 - mine, 1)
            remote(ref, ref, z_send.at[14], z_recv.at[14], z_out).start()
            ref = piece(par, plane(6 * sig), 1 - mine, 0)
            remote(ref, ref, d_send.at[1], d_recv.at[1], y_near).start()

        pass_near(near_here(2 * t + 2), near_here(2 * t + 3))

        @pl.when(t >= 1)
        def _():
            handed(t - 1)
            handed(17 + t - 1)

        @pl.when((t == 1) | (t == 2))
        def _():
            handed(15 + t - 1)

        @pl.when(t >= 2)
        def _():
            handed(32 + t - 2)
            handed(44 + t - 2)

        @pl.when(t == 3)
        def _():
            handed(56)
            handed(57)

        project(t)

    def last(send, recv, step, r, i):
        ref = piece(1 - par, plane(-step * sig), 1 - mine, r)
        arrived(ref, send, recv)
        pass_over(ref, i)

    last(d_send.at[0], d_recv.at[0], 5, 1, 58)
    last(d_send.at[1], d_recv.at[1], 6, 0, 59)
    last(y_send.at[14], y_recv.at[14], 5, 0, 31)
    last(z_send.at[14], z_recv.at[14], 6, 1, 14)
    attend_group(GROUPS - 1)

    for i in (13, 30, 14, 31, 58, 59):
        handed(i)

    project(TICKS)

    def sent(ref, send, recv):
        remote(ref, ref, send, recv, other).wait_send()

    @pl.loop(0, 15)
    def _(i):
        sent(any_piece, z_send.at[i], z_recv.at[i])
        sent(any_piece, y_send.at[i], y_recv.at[i])

    @pl.loop(0, 13)
    def _(i):
        for r in range(2):
            sent(any_piece, x_send.at[r, i], x_recv.at[r, i])

    for i in range(2):
        sent(any_piece, h_send.at[i], h_recv.at[i])
        sent(any_piece, d_send.at[i], d_recv.at[i])

    @pl.loop(0, 60)
    def _(i):
        sent(any_piece, c_send.at[i], c_recv.at[i])

    @pl.loop(0, GROUPS)
    def _(g):
        for which in range(2):
            sent(slot(near, which, g), near_send.at[which, g], near_recv.at[which, g])
            sent(slot(far, which, g), far_send.at[which, g], far_recv.at[which, g])


def local(query_frames, key_frames, value_frames, stream, out_weight):
    dma = pltpu.SemaphoreType.DMA
    bf16 = jnp.bfloat16
    total = pl.pallas_call(
        kernel,
        out_shape=jax.ShapeDtypeStruct((BLOCK, D), jnp.float32),
        in_specs=[pl.BlockSpec(memory_space=pltpu.HBM)] * 5,
        out_specs=pl.BlockSpec(memory_space=pltpu.VMEM),
        scratch_shapes=[
            pltpu.VMEM((BLOCK, WIDTH), bf16),
            pltpu.VMEM((2, BLOCK, WIDTH), bf16),
            pltpu.VMEM((2, BLOCK, WIDTH), bf16),
            pltpu.VMEM((2, BLOCK, WIDTH), bf16),
            pltpu.VMEM((BLOCK, WIDTH), bf16),
            pltpu.VMEM((BLOCK, D), bf16),
            pltpu.VMEM((WIDTH, D), bf16),
            dma((5,)),
            dma((15,)), dma((15,)),
            dma((2,)), dma((2,)),
            dma((15,)), dma((15,)),
            dma((2, 13)), dma((2, 13)),
            dma((2,)), dma((2,)),
            dma((60,)), dma((60,)),
            dma((2, GROUPS)), dma((2, GROUPS)),
            dma((2, GROUPS)), dma((2, GROUPS)),
        ],
        compiler_params=pltpu.CompilerParams(
            collective_id=0, has_side_effects=True, vmem_limit_bytes=44 * 1024 * 1024
        ),
    )(*[pltpu.with_memory_space_constraint(a, pltpu.HBM) for a in (query_frames, key_frames, value_frames, stream, out_weight)])
    return total.astype(bf16)


def solution(mesh):
    in_specs = (
        P(("dp", "ctx"), None),
        P(("dp", "ctx"), None),
        P(("dp", "ctx"), None),
        P(("dp", "ctx"), None),
        P("ctx", None),
    )
    out_specs = P(("dp", "ctx"), None)
    return jax.shard_map(local, mesh=mesh, in_specs=in_specs, out_specs=out_specs, check_vma=False)
```
